32 devices in a mesh: fsdp: 8 (over z, x), rep: 4 (over y, core).
Axes of the slice: x: 2, y: 2, z: 4, core: 2. Of those that a mesh axis runs over, the one named last changes fastest.
Arguments:
- grad: bfloat16 [16, 256, 2048], P(None, 'fsdp'), may hold values from -6 to 6
- momentum: float32 [16, 256, 2048], P(None, 'fsdp'), may hold values from -6 to 6
- owner_list: int32 [16], replicated, may hold values from 0 to 7, as said below
Outputs:
- new_momentum: float32 [16, 256, 2048], P(None, 'fsdp')
- update: bfloat16 [16, 256, 2048], P(None, 'fsdp')
- owned_update: bfloat16 [32, 256, 2048], P(('fsdp', 'rep'))
The draws below stay inside these ranges and needn't reach their ends.
Inputs may be any that keep to these rules, and one draw needn't show every extreme that they name: `owner_list`: no owner is named by more than 4 matrices; some owner is named by exactly 4 in every draw.
All inputs are finite; a program needn't handle non-finite values.
Results may differ from the reference program's by a relative error of at most 0.03.
Values may be sent and summed in bfloat16 or wider, within the bound.
No kernel may reach another device: no remote copies, remote signals or barrier semaphores. Data moves between devices by JAX's collectives and lax.ppermute only.
A program may use at most 128 MiB of HBM per device.

```python
import jax
import jax.numpy as jnp
from jax import lax

ROWS = 256
COLS = 2048
CAP = 4
ITERS = 5
MATS = 16
N_FSDP = 8


def draw_owner_list(key, part):
    first_key, second_key, third_key = jax.random.split(jax.random.fold_in(key, 17), 3)
    order = jax.random.permutation(first_key, N_FSDP)
    halves = jax.random.randint(second_key, (N_FSDP // 2,), 0, CAP + 1).astype(jnp.int32)
    halves = halves.at[0].set(CAP)
    ordered_counts = jnp.stack([halves, CAP - halves], axis=1).reshape(-1).astype(jnp.int32)
    counts = jnp.zeros((N_FSDP,), jnp.int32).at[order].set(ordered_counts)
    ends = jnp.cumsum(counts)
    grouped = jnp.searchsorted(ends, jnp.arange(MATS), side='right').astype(jnp.int32)
    return grouped[jax.random.permutation(third_key, MATS)]


def shard_levels(own_key, extent, cuts, smallest, largest):
    level = 1.0
    for dim, blocks in cuts:
        draws = jax.random.uniform(jax.random.fold_in(jax.random.fold_in(own_key, 6), dim), (blocks,), jnp.float32, smallest / len(cuts), largest / len(cuts))
        level = level * jnp.repeat(jnp.exp(draws), extent[dim] // blocks).reshape((-1,) + (1,) * (len(extent) - 1 - dim))
    return level


def noise(rng, shape, spread, limit, pieces=(), kind=jnp.bfloat16):
    loudness = shard_levels(rng, shape, pieces, -0.22, 0.18) if pieces else 1.0
    result = jax.random.normal(rng, shape, jnp.float32) * spread * loudness
    return jnp.minimum(jnp.maximum(result, -limit), limit).astype(kind)


def setup_inputs(seed: int = 0) -> dict:
    seeds = jax.random.split(jax.random.key(seed), 4)
    grad = noise(seeds[0], (MATS, ROWS, COLS), 1.0, 6.0, ((1, 8),))
    momentum = noise(seeds[1], (MATS, ROWS, COLS), 1.0, 6.0, ((1, 8),), jnp.float32)
    owner_list = draw_owner_list(jax.random.fold_in(seeds[3], 71), 0)
    return dict(grad=grad, momentum=momentum, owner_list=owner_list)


decay_rate = 0.95
norm_eps = 1e-07
quintic_a = 3.4445
quintic_b = -4.775
quintic_c = 2.0315

def newton(blended):
    values = blended.astype(jnp.float32)
    total = jnp.sqrt(jnp.sum(values * values))
    current = (values / (total + norm_eps)).astype(jnp.bfloat16)
    for iteration in range(ITERS):
        gram = jnp.dot(current, current.T, preferred_element_type=jnp.float32).astype(jnp.bfloat16)
        square = jnp.dot(gram, gram, preferred_element_type=jnp.float32)
        poly = (quintic_b * gram.astype(jnp.float32) + quintic_c * square).astype(jnp.bfloat16)
        applied = jnp.dot(poly, current, preferred_element_type=jnp.float32)
        current = (quintic_a * current.astype(jnp.float32) + applied).astype(jnp.bfloat16)
    return current

def reference(grad, momentum, owner_list):
    new_momentum = decay_rate * momentum + grad.astype(jnp.float32)
    blended = (grad.astype(jnp.float32) + decay_rate * new_momentum).astype(jnp.bfloat16)
    update = lax.map(newton, blended)
    order = jnp.arange(MATS)
    earlier = order[None, :] < order[:, None]
    same_owner = owner_list[None, :] == owner_list[:, None]
    slot_index = lax.optimization_barrier(jnp.sum(jnp.logical_and(earlier, same_owner), axis=1)).astype(jnp.int32)
    position = (owner_list * CAP + slot_index).astype(jnp.int32)
    owned_update = jnp.zeros((N_FSDP * CAP, ROWS, COLS), jnp.bfloat16).at[position].set(update)
    return (new_momentum, update, owned_update)
```

```python
import functools

import jax
import jax.numpy as jnp
from jax import lax
from jax.experimental import pallas as pl
from jax.experimental.pallas import tpu as pltpu
from jax.sharding import PartitionSpec as P

CAP = 4
ITERS = 5


decay_rate = 0.95
norm_eps = 1e-07
quintic_a = 3.4445
quintic_b = -4.775
quintic_c = 2.0315


def newton(blended):
    values = blended.astype(jnp.float32)
    total = jnp.sqrt(jnp.sum(values * values))
    current = (values / (total + norm_eps)).astype(jnp.bfloat16)
    for iteration in range(ITERS):
        gram = jnp.dot(current, current.T, preferred_element_type=jnp.float32).astype(jnp.bfloat16)
        square = jnp.dot(gram, gram, preferred_element_type=jnp.float32)
        poly = (quintic_b * gram.astype(jnp.float32) + quintic_c * square).astype(jnp.bfloat16)
        applied = jnp.dot(poly, current, preferred_element_type=jnp.float32)
        current = (quintic_a * current.astype(jnp.float32) + applied).astype(jnp.bfloat16)
    return current


def general(grad, momentum, owner_list):
    matrix_count, row_count, col_count = grad.shape
    owner_count = lax.axis_size("fsdp")
    replicas = lax.axis_size("rep")
    capacity = CAP
    per_replica = capacity // replicas
    replica = lax.axis_index("rep")
    new_momentum = decay_rate * momentum + grad.astype(jnp.float32)
    blended = (grad.astype(jnp.float32) + decay_rate * new_momentum).astype(jnp.bfloat16)
    order = jnp.arange(matrix_count)
    earlier = order[None, :] < order[:, None]
    same_owner = owner_list[None, :] == owner_list[:, None]
    slot_index = jnp.sum(jnp.logical_and(earlier, same_owner), axis=1)
    position = slot_index * owner_count + owner_list
    targets = jnp.arange(capacity * owner_count)
    matched = position[None, :] == targets[:, None]
    sources = jnp.sum(jnp.where(matched, order[None, :], 0), axis=1)
    filled = jnp.any(matched, axis=1)
    flattened = blended.reshape(matrix_count, row_count * col_count)
    first_slot = replica * per_replica
    chosen = lax.dynamic_slice_in_dim(sources, first_slot * owner_count, per_replica * owner_count)
    usable = lax.dynamic_slice_in_dim(filled, first_slot * owner_count, per_replica * owner_count)
    picked = jnp.take(flattened, chosen, axis=0)
    picked = jnp.where(usable[:, None], picked, jnp.zeros_like(picked))
    outgoing = picked.reshape(per_replica, owner_count, row_count, col_count)
    received = lax.all_to_all(outgoing, "fsdp", split_axis=1, concat_axis=1, tiled=True)
    items = received.shape[0]
    matrices = received.reshape(items, owner_count * row_count, col_count)
    result = jax.vmap(newton)(matrices)
    finished = result.reshape(items, owner_count, row_count, col_count)
    owned_update = finished.reshape(per_replica, owner_count * row_count, col_count)
    returned = lax.all_to_all(finished, "fsdp", split_axis=1, concat_axis=1, tiled=True)
    complete = lax.all_gather(returned, "rep", axis=0, tiled=True)
    stacked = complete.reshape(capacity * owner_count, row_count, col_count)
    update = jnp.take(stacked, position, axis=0)
    return (new_momentum, update, owned_update)


def assign_slots(owner, matrices, owners, count_ref, spare_ref, assign_ref, home_ref):
    half = owners // 2
    places = half * CAP
    for o in range(owners):
        count_ref[o] = 0
    for p in range(owners * CAP):
        assign_ref[p] = -1
    spare = [jnp.int32(0), jnp.int32(0)]
    for m in range(matrices):
        o = owner[m]
        slot = count_ref[o]
        count_ref[o] = slot + 1
        assign_ref[o * CAP + slot] = m
        upper = (o >= half).astype(jnp.int32)
        spare_ref[upper * matrices + jnp.where(upper == 1, spare[1], spare[0])] = m
        spare = [spare[0] + (1 - upper), spare[1] + upper]
    filled = []
    taken = [jnp.int32(0), jnp.int32(0)]
    for p in range(places):
        for h in range(2):
            q = h * places + p
            held = assign_ref[q]
            empty = held < 0
            other = spare_ref[(1 - h) * matrices + jnp.minimum(taken[h], matrices - 1)]
            m = jnp.where(empty, other, held)
            taken[h] = taken[h] + empty.astype(jnp.int32)
            assign_ref[q] = jnp.where(empty, m - 2 * matrices, m)
            home_ref[h * matrices + m] = q


def blend_kernel(owners, matrices, owner_ref, grad_ref, momentum_ref, *rest):
    outs, (home_out, filled_out) = rest[:owners], rest[owners : owners + 2]
    grads, momenta, count_ref, spare_ref, assign_ref, home_ref, sems = rest[owners + 2 :]
    f, r = lax.axis_index("fsdp"), lax.axis_index("rep")
    assign_slots(owner_ref, matrices, owners, count_ref, spare_ref, assign_ref, home_ref)
    order = list(range(owners - 1, -1, -1))
    copies = []
    for k in order:
        held = assign_ref[(f ^ k) * CAP + r]
        m = jnp.where(held < 0, held + 2 * matrices, held)
        g = pltpu.make_async_copy(grad_ref.at[m], grads.at[k], sems.at[0, k])
        v = pltpu.make_async_copy(momentum_ref.at[m], momenta.at[k], sems.at[1, k])
        g.start()
        v.start()
        copies.append((g, v))
    half = (f >= owners // 2).astype(jnp.int32)
    for m in range(matrices):
        home_out[m] = home_ref[half * matrices + m]
    filled_out[0] = (assign_ref[f * CAP + r] >= 0).astype(jnp.int32)
    for k, (g, v) in zip(order, copies):
        g.wait()
        v.wait()
        gradient = grads[k].astype(jnp.float32)
        fresh = decay_rate * momenta[k] + gradient
        outs[k][...] = (gradient + decay_rate * fresh).astype(jnp.bfloat16)


def blend(grad, momentum, owner_list, owners):
    matrices, rows, cols = grad.shape
    block = jax.ShapeDtypeStruct((rows, cols), jnp.bfloat16)
    whole = pl.BlockSpec(memory_space=pltpu.VMEM)
    scalars = pl.BlockSpec(memory_space=pltpu.SMEM)
    outs = pl.pallas_call(
        functools.partial(blend_kernel, owners, matrices),
        out_shape=[block] * owners + [jax.ShapeDtypeStruct((matrices,), jnp.int32), jax.ShapeDtypeStruct((1,), jnp.int32)],
        in_specs=[scalars, pl.BlockSpec(memory_space=pltpu.HBM), pl.BlockSpec(memory_space=pltpu.HBM)],
        out_specs=[whole] * owners + [scalars] * 2,
        scratch_shapes=[
            pltpu.VMEM((owners, rows, cols), jnp.bfloat16),
            pltpu.VMEM((owners, rows, cols), jnp.float32),
            pltpu.SMEM((owners,), jnp.int32),
            pltpu.SMEM((2 * matrices,), jnp.int32),
            pltpu.SMEM((owners * CAP,), jnp.int32),
            pltpu.SMEM((2 * matrices,), jnp.int32),
            pltpu.SemaphoreType.DMA((2, owners)),
        ],
        compiler_params=pltpu.CompilerParams(vmem_limit_bytes=12 << 20),
        name="blend",
    )(owner_list, grad, momentum)
    return outs[:owners], outs[owners], outs[owners + 1]


def newton_kernel(owners, filled_ref, *rest):
    blocks, owned_ref, outs = rest[:owners], rest[owners], rest[owners + 1 : owners + 1 + owners // 2]
    current_ref = rest[-1]
    rows, cols = blocks[0].shape
    f = lax.axis_index("fsdp")
    total = jnp.zeros((rows, cols), jnp.float32)
    for k in range(owners):
        values = blocks[k][...].astype(jnp.float32)
        total = total + values * values
    scale = 1.0 / (jnp.sqrt(jnp.sum(total)) + norm_eps)
    for k in range(owners):
        start = pl.multiple_of((f ^ k) * rows, rows)
        current_ref[pl.ds(start, rows), :] = (blocks[k][...].astype(jnp.float32) * scale).astype(jnp.bfloat16)
    for iteration in range(ITERS):
        current = current_ref[...]
        gram = lax.dot_general(current, current, (((1,), (1,)), ((), ())), preferred_element_type=jnp.float32).astype(jnp.bfloat16)
        square = jnp.dot(gram, gram, preferred_element_type=jnp.float32)
        poly = (quintic_b * gram.astype(jnp.float32) + quintic_c * square).astype(jnp.bfloat16)
        applied = jnp.dot(poly, current, preferred_element_type=jnp.float32)
        current_ref[...] = (quintic_a * current.astype(jnp.float32) + applied).astype(jnp.bfloat16)
    for k in range(owners // 2):
        start = pl.multiple_of((f ^ k) * rows, rows)
        outs[k][...] = current_ref[pl.ds(start, rows), :]
    owned_ref[...] = jnp.where(filled_ref[0] > 0, current_ref[...], jnp.zeros_like(current_ref))


def orthogonalize(blocks, filled):
    owners = len(blocks)
    rows, cols = blocks[0].shape
    whole = pl.BlockSpec(memory_space=pltpu.VMEM)
    outs = pl.pallas_call(
        functools.partial(newton_kernel, owners),
        out_shape=[jax.ShapeDtypeStruct((owners * rows, cols), jnp.bfloat16)]
        + [jax.ShapeDtypeStruct((rows, cols), jnp.bfloat16)] * (owners // 2),
        in_specs=[pl.BlockSpec(memory_space=pltpu.SMEM)] + [whole] * owners,
        out_specs=[whole] * (1 + owners // 2),
        scratch_shapes=[pltpu.VMEM((owners * rows, cols), jnp.bfloat16)],
        compiler_params=pltpu.CompilerParams(vmem_limit_bytes=16 << 20),
        name="newton",
    )(filled, *blocks)
    return outs[0], outs[1:]


def place_kernel(matrices, count, keys, home_ref, *rest):
    blocks, out_ref, source_ref, sems = rest[:count], rest[count], rest[count + 1], rest[count + 2]
    f, r = lax.axis_index("fsdp"), lax.axis_index("rep")
    for m in range(matrices):
        source_ref[home_ref[m]] = m
    copies = []
    for i, (kf, kr) in enumerate(keys):
        m = source_ref[(f ^ kf) * CAP + (r ^ kr)]
        copy = pltpu.make_async_copy(blocks[i], out_ref.at[m], sems.at[i])
        copy.start()
        copies.append(copy)
    for copy in copies:
        copy.wait()


def place(home, blocks, keys, owners):
    matrices = home.shape[0]
    rows, cols = blocks[0].shape
    return pl.pallas_call(
        functools.partial(place_kernel, matrices, len(blocks), keys),
        out_shape=jax.ShapeDtypeStruct((matrices, rows, cols), jnp.bfloat16),
        in_specs=[pl.BlockSpec(memory_space=pltpu.SMEM)] + [pl.BlockSpec(memory_space=pltpu.VMEM)] * len(blocks),
        out_specs=pl.BlockSpec(memory_space=pl.ANY),
        scratch_shapes=[pltpu.SMEM((owners * CAP,), jnp.int32), pltpu.SemaphoreType.DMA((len(blocks),))],
        compiler_params=pltpu.CompilerParams(vmem_limit_bytes=8 << 20),
        name="place",
    )(home, *blocks)


def swap(block, kf, kr):
    owners, replicas = lax.axis_size("fsdp"), lax.axis_size("rep")
    pairs = [
        (o * replicas + p, (o ^ kf) * replicas + (p ^ kr)) for o in range(owners) for p in range(replicas)
    ]
    return lax.ppermute(block, ("fsdp", "rep"), pairs)


def halves(grad, momentum, owner_list):
    owners, replicas = lax.axis_size("fsdp"), lax.axis_size("rep")
    outgoing, home, filled = blend(grad, momentum, owner_list, owners)
    received = [outgoing[0]] + [None] * (owners - 1)
    for k in range(owners - 1, 0, -1):
        received[k] = swap(outgoing[k], k, 0)
    new_momentum = decay_rate * momentum + grad.astype(jnp.float32)
    new_momentum, filled = lax.optimization_barrier((new_momentum, filled))
    owned, results = orthogonalize(received, filled)
    pieces = {}
    for kf in range(owners // 2 - 1, -1, -1):
        for kr in range(0, replicas, 2):
            pieces[kf, kr] = results[0] if kf == kr == 0 else swap(results[kf], kf, kr)
    for kf, kr in list(pieces):
        pieces[kf, kr + 1] = swap(pieces[kf, kr], 0, 1)
    keys = tuple(pieces)
    update = place(home, [pieces[key] for key in keys], keys, owners)
    return (new_momentum, update, owned[None])


def solution(mesh):
    in_specs = (P(None, "fsdp", None), P(None, "fsdp", None), P())
    out_specs = (P(None, "fsdp", None), P(None, "fsdp", None), P(("fsdp", "rep"), None, None))
    owners, replicas = mesh.shape["fsdp"], mesh.shape["rep"]

    def local(grad, momentum, owner_list):
        matrices, rows, cols = grad.shape
        small = owners & (owners - 1) == 0 and 2 <= owners <= 8
        paired = replicas == CAP and matrices == owners // 2 * replicas
        tiled = rows % 16 == 0 and cols % 128 == 0
        chosen = halves if small and paired and tiled else general
        return chosen(grad, momentum, owner_list)

    return jax.shard_map(local, mesh=mesh, in_specs=in_specs, out_specs=out_specs, check_vma=False)
```

```python
import functools

import jax
import jax.numpy as jnp
from jax import lax
from jax.experimental import pallas as pl
from jax.experimental.pallas import tpu as pltpu
from jax.sharding import PartitionSpec as P

CAP = 4
ITERS = 5


decay_rate = 0.95
norm_eps = 1e-07
quintic_a = 3.4445
quintic_b = -4.775
quintic_c = 2.0315


def newton(blended):
    values = blended.astype(jnp.float32)
    total = jnp.sqrt(jnp.sum(values * values))
    current = (values / (total + norm_eps)).astype(jnp.bfloat16)
    for iteration in range(ITERS):
        gram = jnp.dot(current, current.T, preferred_element_type=jnp.float32).astype(jnp.bfloat16)
        square = jnp.dot(gram, gram, preferred_element_type=jnp.float32)
        poly = (quintic_b * gram.astype(jnp.float32) + quintic_c * square).astype(jnp.bfloat16)
        applied = jnp.dot(poly, current, preferred_element_type=jnp.float32)
        current = (quintic_a * current.astype(jnp.float32) + applied).astype(jnp.bfloat16)
    return current


def general(grad, momentum, owner_list):
    matrix_count, row_count, col_count = grad.shape
    owner_count = lax.axis_size("fsdp")
    replicas = lax.axis_size("rep")
    capacity = CAP
    per_replica = capacity // replicas
    replica = lax.axis_index("rep")
    new_momentum = decay_rate * momentum + grad.astype(jnp.float32)
    blended = (grad.astype(jnp.float32) + decay_rate * new_momentum).astype(jnp.bfloat16)
    order = jnp.arange(matrix_count)
    earlier = order[None, :] < order[:, None]
    same_owner = owner_list[None, :] == owner_list[:, None]
    slot_index = jnp.sum(jnp.logical_and(earlier, same_owner), axis=1)
    position = slot_index * owner_count + owner_list
    targets = jnp.arange(capacity * owner_count)
    matched = position[None, :] == targets[:, None]
    sources = jnp.sum(jnp.where(matched, order[None, :], 0), axis=1)
    filled = jnp.any(matched, axis=1)
    flattened = blended.reshape(matrix_count, row_count * col_count)
    first_slot = replica * per_replica
    chosen = lax.dynamic_slice_in_dim(sources, first_slot * owner_count, per_replica * owner_count)
    usable = lax.dynamic_slice_in_dim(filled, first_slot * owner_count, per_replica * owner_count)
    picked = jnp.take(flattened, chosen, axis=0)
    picked = jnp.where(usable[:, None], picked, jnp.zeros_like(picked))
    outgoing = picked.reshape(per_replica, owner_count, row_count, col_count)
    received = lax.all_to_all(outgoing, "fsdp", split_axis=1, concat_axis=1, tiled=True)
    items = received.shape[0]
    matrices = received.reshape(items, owner_count * row_count, col_count)
    result = jax.vmap(newton)(matrices)
    finished = result.reshape(items, owner_count, row_count, col_count)
    owned_update = finished.reshape(per_replica, owner_count * row_count, col_count)
    returned = lax.all_to_all(finished, "fsdp", split_axis=1, concat_axis=1, tiled=True)
    complete = lax.all_gather(returned, "rep", axis=0, tiled=True)
    stacked = complete.reshape(capacity * owner_count, row_count, col_count)
    update = jnp.take(stacked, position, axis=0)
    return (new_momentum, update, owned_update)


def assign_slots(owner, matrices, owners, count_ref, spare_ref, assign_ref, home_ref):
    half = owners // 2
    places = half * CAP
    for o in range(owners):
        count_ref[o] = 0
    for p in range(owners * CAP):
        assign_ref[p] = -1
    spare = [jnp.int32(0), jnp.int32(0)]
    for m in range(matrices):
        o = owner[m]
        slot = count_ref[o]
        count_ref[o] = slot + 1
        assign_ref[o * CAP + slot] = m
        upper = (o >= half).astype(jnp.int32)
        spare_ref[upper * matrices + jnp.where(upper == 1, spare[1], spare[0])] = m
        spare = [spare[0] + (1 - upper), spare[1] + upper]
    filled = []
    taken = [jnp.int32(0), jnp.int32(0)]
    for p in range(places):
        for h in range(2):
            q = h * places + p
            held = assign_ref[q]
            empty = held < 0
            other = spare_ref[(1 - h) * matrices + jnp.minimum(taken[h], matrices - 1)]
            m = jnp.where(empty, other, held)
            taken[h] = taken[h] + empty.astype(jnp.int32)
            assign_ref[q] = jnp.where(empty, m - 2 * matrices, m)
            home_ref[h * matrices + m] = q


def blend_kernel(matrices, ks, first, *rest):
    table_ref, grad_ref, momentum_ref, *rest = rest
    outs, rest = rest[: len(ks)], rest[len(ks) :]
    f, r = lax.axis_index("fsdp"), lax.axis_index("rep")
    if first:
        owners = lax.axis_size("fsdp")
        assign_ref, home_ref, filled_ref, *rest = rest
        count_ref, spare_ref, *rest = rest
        assign_slots(table_ref, matrices, owners, count_ref, spare_ref, assign_ref, home_ref)
        filled_ref[0] = (assign_ref[f * CAP + r] >= 0).astype(jnp.int32)
    else:
        assign_ref = table_ref
    grads, momenta, blended, sems, out_sems = rest
    copies = []
    for i, k in enumerate(ks):
        held = assign_ref[(f ^ k) * CAP + r]
        m = jnp.where(held < 0, held + 2 * matrices, held)
        g = pltpu.make_async_copy(grad_ref.at[m], grads.at[i], sems.at[0, i])
        v = pltpu.make_async_copy(momentum_ref.at[m], momenta.at[i], sems.at[1, i])
        g.start()
        v.start()
        copies.append((g, v))
    written = []
    for i, (g, v) in enumerate(copies):
        g.wait()
        v.wait()
        gradient = grads[i].astype(jnp.float32)
        fresh = decay_rate * momenta[i] + gradient
        blended[i] = (gradient + decay_rate * fresh).astype(jnp.bfloat16)
        out = pltpu.make_async_copy(blended.at[i], outs[i], out_sems.at[i])
        out.start()
        written.append(out)
    for out in written:
        out.wait()


def blend(grad, momentum, table, ks, first, owners):
    matrices, rows, cols = grad.shape
    block = jax.ShapeDtypeStruct((rows, cols), jnp.bfloat16)
    scalars = pl.BlockSpec(memory_space=pltpu.SMEM)
    stay = pl.BlockSpec(memory_space=pl.ANY)
    count = len(ks)
    tables = [(owners * CAP,), (2 * matrices,), (1,)] if first else []
    return pl.pallas_call(
        functools.partial(blend_kernel, matrices, ks, first),
        out_shape=[block] * count + [jax.ShapeDtypeStruct(shape, jnp.int32) for shape in tables],
        in_specs=[scalars, stay, stay],
        out_specs=[stay] * count + [scalars] * len(tables),
        scratch_shapes=[pltpu.SMEM((owners,), jnp.int32), pltpu.SMEM((2 * matrices,), jnp.int32)] * first
        + [
            pltpu.VMEM((count, rows, cols), jnp.bfloat16),
            pltpu.VMEM((count, rows, cols), jnp.float32),
            pltpu.VMEM((count, rows, cols), jnp.bfloat16),
            pltpu.SemaphoreType.DMA((2, count)),
            pltpu.SemaphoreType.DMA((count,)),
        ],
        compiler_params=pltpu.CompilerParams(vmem_limit_bytes=66000000),
        name="blend",
    )(table, grad, momentum)


def newton_kernel(owners, *rest):
    blocks, current_ref, outs = rest[:owners], rest[owners], rest[owners + 1 :]
    rows, cols = blocks[0].shape
    width = min(cols, owners * rows)
    chunks = [slice(start, start + width) for start in range(0, cols, width)]
    f = lax.axis_index("fsdp")
    total = jnp.zeros((rows, cols), jnp.float32)
    for k in range(owners):
        values = blocks[k][...].astype(jnp.float32)
        total = total + values * values
    scale = 1.0 / (jnp.sqrt(jnp.sum(total)) + norm_eps)
    for k in range(owners):
        start = pl.multiple_of((f ^ k) * rows, rows)
        current_ref[pl.ds(start, rows), :] = (blocks[k][...].astype(jnp.float32) * scale).astype(jnp.bfloat16)

    def product(part):
        return lax.dot_general(part, part, (((1,), (1,)), ((), ())), preferred_element_type=jnp.float32)

    gram = sum(product(current_ref[:, chunk]) for chunk in chunks)
    for iteration in range(ITERS):
        gram = gram.astype(jnp.bfloat16)
        square = jnp.dot(gram, gram, preferred_element_type=jnp.float32)
        poly = (quintic_b * gram.astype(jnp.float32) + quintic_c * square).astype(jnp.bfloat16)
        gram = jnp.zeros(gram.shape, jnp.float32)
        for chunk in chunks:
            part = current_ref[:, chunk]
            applied = jnp.dot(poly, part, preferred_element_type=jnp.float32)
            part = (quintic_a * part.astype(jnp.float32) + applied).astype(jnp.bfloat16)
            current_ref[:, chunk] = part
            if iteration < ITERS - 1:
                gram = gram + product(part)
    for k in range(owners // 2):
        start = pl.multiple_of((f ^ k) * rows, rows)
        outs[k][...] = current_ref[pl.ds(start, rows), :]


def orthogonalize(blocks):
    owners = len(blocks)
    rows, cols = blocks[0].shape
    whole = pl.BlockSpec(memory_space=pltpu.VMEM)
    outs = pl.pallas_call(
        functools.partial(newton_kernel, owners),
        out_shape=[jax.ShapeDtypeStruct((owners * rows, cols), jnp.bfloat16)]
        + [jax.ShapeDtypeStruct((rows, cols), jnp.bfloat16)] * (owners // 2),
        in_specs=[whole] * owners,
        out_specs=[whole] * (1 + owners // 2),
        compiler_params=pltpu.CompilerParams(vmem_limit_bytes=16 << 20),
        name="newton",
    )(*blocks)
    return outs[0], outs[1:]


def place_kernel(matrices, count, keys, home_ref, *rest):
    blocks, (out_ref, source_ref, sems) = rest[:count], rest[-3:]
    f, r = lax.axis_index("fsdp"), lax.axis_index("rep")
    upper = (f >= lax.axis_size("fsdp") // 2).astype(jnp.int32)
    for m in range(matrices):
        source_ref[home_ref[upper * matrices + m]] = m
    copies = []
    for i, (kf, kr) in enumerate(keys):
        m = source_ref[(f ^ kf) * CAP + (r ^ kr)]
        copy = pltpu.make_async_copy(blocks[i], out_ref.at[m], sems.at[i])
        copy.start()
        copies.append(copy)
    for copy in copies:
        copy.wait()


def place(homes, pieces, update, owners):
    keys, blocks = tuple(pieces), list(pieces.values())
    rows, cols = blocks[0].shape
    matrices = homes.shape[0] // 2
    earlier = [] if update is None else [update]
    return pl.pallas_call(
        functools.partial(place_kernel, matrices, len(blocks), keys),
        out_shape=jax.ShapeDtypeStruct((matrices, rows, cols), jnp.bfloat16),
        in_specs=[pl.BlockSpec(memory_space=pltpu.SMEM)]
        + [pl.BlockSpec(memory_space=pltpu.VMEM)] * len(blocks)
        + [pl.BlockSpec(memory_space=pl.ANY)] * len(earlier),
        out_specs=pl.BlockSpec(memory_space=pl.ANY),
        scratch_shapes=[pltpu.SMEM((owners * CAP,), jnp.int32), pltpu.SemaphoreType.DMA((len(blocks),))],
        input_output_aliases={1 + len(blocks): 0} if earlier else {},
        compiler_params=pltpu.CompilerParams(vmem_limit_bytes=8 << 20),
        name="place",
    )(homes, *blocks, *earlier)


def swap(block, kf, kr):
    owners, replicas = lax.axis_size("fsdp"), lax.axis_size("rep")
    pairs = [
        (o * replicas + p, (o ^ kf) * replicas + (p ^ kr)) for o in range(owners) for p in range(replicas)
    ]
    return lax.ppermute(block, ("fsdp", "rep"), pairs)


def halves(grad, momentum, owner_list):
    owners, replicas = lax.axis_size("fsdp"), lax.axis_size("rep")
    far, near = tuple(range(owners - 1, owners // 2 - 1, -1)), tuple(range(owners // 2 - 1, -1, -1))
    *outgoing, assign, homes, filled = blend(grad, momentum, owner_list, far, True, owners)
    outgoing += blend(grad, momentum, assign, near, False, owners)
    received = {k: swap(block, k, 0) if k else block for k, block in zip(far + near, outgoing)}
    new_momentum = decay_rate * momentum + grad.astype(jnp.float32)
    new_momentum, received[0] = lax.optimization_barrier((new_momentum, received[0]))
    finished, results = orthogonalize([received[k] for k in range(owners)])
    pieces = {}
    for kf in range(owners // 2 - 1, -1, -1):
        for kr in range(0, replicas, 2):
            pieces[kf, kr] = results[0] if kf == kr == 0 else swap(results[kf], kf, kr)
    owned = jnp.where(filled[0] > 0, finished, jnp.zeros_like(finished))
    leaving = dict(pieces)
    first = next(iter(leaving))
    owned, leaving[first] = lax.optimization_barrier((owned, leaving[first]))
    others = {(kf, kr + 1): swap(block, 0, 1) for (kf, kr), block in leaving.items()}
    update = place(homes, others, place(homes, pieces, None, owners), owners)
    return (new_momentum, update, owned[None])


def solution(mesh):
    in_specs = (P(None, "fsdp", None), P(None, "fsdp", None), P())
    out_specs = (P(None, "fsdp", None), P(None, "fsdp", None), P(("fsdp", "rep"), None, None))
    owners, replicas = mesh.shape["fsdp"], mesh.shape["rep"]

    def local(grad, momentum, owner_list):
        matrices, rows, cols = grad.shape
        small = owners & (owners - 1) == 0 and 2 <= owners <= 8
        paired = replicas == CAP and matrices == owners // 2 * replicas
        tiled = rows % 16 == 0 and cols % 128 == 0
        chosen = halves if small and paired and tiled else general
        return chosen(grad, momentum, owner_list)

    return jax.shard_map(local, mesh=mesh, in_specs=in_specs, out_specs=out_specs, check_vma=False)
```
